32 devices in a mesh: own: 8 (over z, x), grp: 4 (over y, core).
Axes of the slice: x: 2, y: 2, z: 4, core: 2. Of those that a mesh axis runs over, the one named last changes fastest.
Arguments:
- panel: float32 [8, 4, 768, 768], P('own', 'grp'), may hold values from -6 to 6
- diag_inverse: float32 [8, 768, 768], P('own', 'grp'), as said below
- ancestor: float32 [8, 4, 768, 768], P('own', 'grp'), may hold values from -6 to 6
- live_blocks: int32 [8], P('own'), may hold values from 1 to 4
- pair_first: int32 [8, 4, 7], P('own', 'grp'), may hold values from 0 to 3
- pair_second: int32 [8, 4, 7], P('own', 'grp'), may hold values from 0 to 3
- pair_offset: int32 [8, 4, 7], P('own', 'grp'), may hold values from 0 to 4
Outputs:
- solved: float32 [8, 4, 768, 768], P('own', 'grp')
- updated: float32 [8, 4, 768, 768], P('own', 'grp')
The draws below stay inside these ranges and needn't reach their ends.
Inputs may be any that keep to these rules, and one draw needn't show every extreme that they name: diag_inverse[s] is upper triangular with a positive diagonal.
All inputs are finite; a program needn't handle non-finite values.
Results may differ from the reference program's by a relative error of at most 0.0001.
Values sent between devices are 32-bit elements; how exact they have to be, the bound alone decides.
No kernel may reach another device: no remote copies, remote signals or barrier semaphores. Data moves between devices by JAX's collectives and lax.ppermute only.
A program may use at most 128 MiB of HBM per device.

```python
import math
import jax
import jax.numpy as jnp
import numpy as np
from jax import lax

B = 768
PAIRS = 7
REACH = 5
SUPERS = 8
N_GRP = 4


def draw_diag_inverse(key, part):
    first_key, second_key = jax.random.split(jax.random.fold_in(key, 71))
    factor = B ** (-0.25)
    diagonal = jax.random.uniform(first_key, (SUPERS, B), jnp.float32, 0.5, 1.0) * factor
    upper = jax.random.normal(second_key, (SUPERS, B, B), jnp.float32) * (factor / B ** 0.5)
    strict = jnp.triu(jnp.ones((B, B), jnp.float32), 1)
    return upper * strict[None] + diagonal[:, :, None] * jnp.eye(B, dtype=jnp.float32)[None]


def touch_ends(entries, stream_key, smallest, high):
    longest = entries.shape.index(max(entries.shape))
    spots = []
    for shift in (0, 1):
        where = [jax.random.randint(jax.random.fold_in(stream_key, axis), (), 0, length) for axis, length in enumerate(entries.shape)]
        where[longest] = (where[longest] + shift) % entries.shape[longest]
        spots.append(tuple(where))
    return entries.at[spots[0]].set(smallest).at[spots[1]].set(high)


def steps_of(own_key, dims, shards, low, largest):
    def one(axis_at, parts):
        heights = jax.random.uniform(jax.random.fold_in(jax.random.fold_in(own_key, 6), axis_at), (parts,), jnp.float32, low / len(shards), largest / len(shards))
        return jnp.repeat(jnp.exp(heights), dims[axis_at] // parts).reshape((-1,) + (1,) * (len(dims) - axis_at - 1))

    factor_of = one(*shards[0])
    for cut in shards[1:]:
        factor_of = factor_of * one(*cut)
    return factor_of


def rank_bounds(count, skew):
    portions = [(1 << 20) // math.isqrt(grade ** skew) + 1 for grade in range(1, count + 1)]
    spread = 1 + sum(portions) // (1 << 30)
    return np.cumsum(np.array([max(1, weight // spread) for weight in portions]))


def ranked_ids(stream_key, shape, count, skew):
    table = rank_bounds(count, skew)
    lot = jax.random.randint(jax.random.fold_in(stream_key, 1), shape, 0, int(table[count - 1]))
    standing = jnp.searchsorted(jnp.asarray(table, jnp.int32), lot, side="right")
    return jax.random.permutation(jax.random.fold_in(stream_key, 2), count)[standing].astype(jnp.int32)


def bell_draw(rng, shape, spread, reach, cuts=(), kind=jnp.bfloat16):
    result = jax.random.normal(rng, shape, jnp.float32) * spread
    if len(cuts) > 0:
        result = steps_of(rng, shape, cuts, -0.22, 0.18) * result
    return jnp.clip(result, min=-reach, max=reach).astype(kind)


def setup_inputs(seed: int = 0) -> dict:
    arg_keys = jax.random.split(jax.random.key(seed), 8)
    panel = bell_draw(arg_keys[0], (SUPERS, N_GRP, B, B), 1.0, 6.0, ((0, 8), (1, 4)), jnp.float32)
    diag_inverse = draw_diag_inverse(jax.random.fold_in(arg_keys[7], 71), 0)
    ancestor = bell_draw(arg_keys[2], (SUPERS, N_GRP, B, B), 1.0, 6.0, ((0, 8), (1, 4)), jnp.float32)
    live_blocks = touch_ends(jax.random.randint(arg_keys[3], (SUPERS,), 1, N_GRP + 1), jax.random.fold_in(arg_keys[3], 1), 1, N_GRP).astype(jnp.int32)
    pair_first = touch_ends(jax.random.randint(arg_keys[4], (SUPERS, N_GRP, PAIRS), 0, N_GRP), jax.random.fold_in(arg_keys[4], 1), 0, N_GRP - 1).astype(jnp.int32)
    pair_second = touch_ends(jax.random.randint(arg_keys[5], (SUPERS, N_GRP, PAIRS), 0, N_GRP), jax.random.fold_in(arg_keys[5], 1), 0, N_GRP - 1).astype(jnp.int32)
    pair_offset = touch_ends(ranked_ids(arg_keys[6], (SUPERS, N_GRP, PAIRS), REACH, 2), jax.random.fold_in(arg_keys[6], 3), 0, REACH - 1).astype(jnp.int32)
    return {"panel": panel, "diag_inverse": diag_inverse, "ancestor": ancestor, "live_blocks": live_blocks, "pair_first": pair_first, "pair_second": pair_second, "pair_offset": pair_offset}


def reference(panel, diag_inverse, ancestor, live_blocks, pair_first, pair_second, pair_offset):
    groups = panel.shape[1]
    alive = (jnp.arange(groups, dtype=jnp.int32)[None, :] < live_blocks[:, None]).astype(panel.dtype)
    solved = jnp.einsum("sgij,sjk->sgik", panel, diag_inverse, precision=lax.Precision.HIGHEST)
    solved = solved * alive[:, :, None, None]
    supers = panel.shape[0]

    def one_super(index, updated):
        column = solved[index]
        first = column[pair_first[index]]
        second = column[pair_second[index]]
        terms = jnp.einsum("gpij,gpkj->gpik", first, second, precision=lax.Precision.HIGHEST)
        for distance in range(REACH):
            weights = (pair_offset[index] == distance).astype(terms.dtype)
            contrib = jnp.einsum("gp,gpik->gik", weights, terms, precision=lax.Precision.HIGHEST)
            target = ((index + distance) % supers).astype(jnp.int32)
            current = lax.dynamic_index_in_dim(updated, target, 0, keepdims=False)
            updated = lax.dynamic_update_index_in_dim(updated, current - contrib, target, 0)
        return updated

    updated = lax.fori_loop(0, supers, one_super, ancestor)
    return solved, updated
```

```python
import jax
import jax.numpy as jnp
from jax import lax
from jax.experimental import pallas as pl
from jax.experimental.pallas import tpu as pltpu
from jax.sharding import PartitionSpec as P


REACH = 5
CHUNKS = 3
GRANT = 40 * 2**20
IN_VMEM = pl.BlockSpec(memory_space=pltpu.VMEM)
IN_SMEM = pl.BlockSpec(memory_space=pltpu.SMEM)


def swapped(array, axis, by):
    size = lax.axis_size(axis)
    return lax.ppermute(array, axis, [(i, i ^ by) for i in range(size)])


def passed_along(array, axis, by):
    size = lax.axis_size(axis)
    return lax.ppermute(array, axis, [(i, (i + by) % size) for i in range(size)])


def everyone(array, axis):
    size = lax.axis_size(axis)
    held = {0: array}
    bit = size // 2
    while bit:
        for r in sorted(held):
            held[r ^ bit] = swapped(held[r], axis, bit)
        bit //= 2
    return [held[r] for r in range(size)]


def halves(value):
    high = value.astype(jnp.bfloat16)
    low = (value - high.astype(jnp.float32)).astype(jnp.bfloat16)
    return high, low


def dot(a, b, dims):
    return lax.dot_general(a, b, (dims, ((), ())), preferred_element_type=jnp.float32)


def product(a, b, dims):
    return dot(a[0], b[0], dims) + (dot(a[0], b[1], dims) + dot(a[1], b[0], dims))


def params(limit=GRANT):
    return pltpu.CompilerParams(vmem_limit_bytes=limit)


def factor_kernel(n, meta, *refs):
    factors, (high_out, low_out) = refs[:n], refs[n:]
    depth = factors[0].shape[0]
    for r in range(n):
        rows = pl.ds(pl.multiple_of((meta[0] ^ r) * depth, depth), depth)
        high_out[rows, :], low_out[rows, :] = halves(factors[r][...])


def split_factor(meta, factors):
    n, order = len(factors), factors[0].shape[1]
    return pl.pallas_call(
        lambda *refs: factor_kernel(n, *refs),
        out_shape=[pltpu.VMEM((order, order), jnp.bfloat16)] * 2,
        in_specs=[IN_SMEM] + [IN_VMEM] * n,
        out_specs=[IN_VMEM] * 2,
        cost_estimate=pl.CostEstimate(flops=order * order, bytes_accessed=8 * order * order, transcendentals=0),
        compiler_params=params(),
        name="factor",
    )(meta, *factors)


def solve_kernel(n, meta, *refs):
    panels, (f_high, f_low), (solved, high_out, low_out) = refs[:n], refs[n : n + 2], refs[-3:]
    _, order = panels[0].shape
    for r in range(n):
        alive = (meta[0] ^ r) < meta[1]
        high, low = halves(panels[r][...])
        for j in range(CHUNKS):
            upto, cols = slice(0, (j + 1) * (order // CHUNKS)), pl.ds(j * (order // CHUNKS), order // CHUNKS)
            value = product((high[:, upto], low[:, upto]), (f_high[upto, cols], f_low[upto, cols]), ((1,), (0,)))
            value = jnp.where(alive, value, 0.0)
            if r == 0:
                solved[:, cols] = value
            high_out[r, :, cols], low_out[r, :, cols] = halves(value)


def solve(meta, panels, factor):
    n = len(panels)
    rows, order = panels[0].shape
    return pl.pallas_call(
        lambda *refs: solve_kernel(n, *refs),
        out_shape=[jax.ShapeDtypeStruct((rows, order), jnp.float32)] + [pltpu.VMEM((n, rows, order), jnp.bfloat16)] * 2,
        in_specs=[IN_SMEM] + [IN_VMEM] * (n + 2),
        out_specs=[IN_VMEM] * 3,
        cost_estimate=pl.CostEstimate(flops=4 * n * rows * order * order, bytes_accessed=8 * n * rows * order, transcendentals=0),
        compiler_params=params(),
        name="solve",
    )(meta, *panels, *factor)


def pair_kernel(left, right, pieces, pairs, *refs):
    highs, lows = refs[:pieces], refs[pieces : 2 * pieces]
    outs, total = refs[2 * pieces : 2 * pieces + REACH], refs[-1]
    count = pairs.shape[0] // 3
    total[...] = jnp.zeros_like(total)

    def stacked(refs, at, block):
        return jnp.concatenate([refs[k][block] for k in at]) if len(at) > 1 else refs[at[0]][block]

    def body(p, carry):
        a, b, d = pairs[p], pairs[count + p], pairs[2 * count + p]
        total[d] += product(
            (stacked(highs, left, a), stacked(lows, left, a)),
            (stacked(highs, right, b), stacked(lows, right, b)),
            ((1,), (1,)),
        )
        return carry

    lax.fori_loop(0, count, body, 0)
    for d in range(REACH):
        outs[d][...] = total[d]


def pair_sums(pairs, highs, lows, left, right):
    pieces, (_, rows, order) = len(highs), highs[0].shape
    shape = (len(left) * rows, len(right) * rows)
    return pl.pallas_call(
        lambda *refs: pair_kernel(left, right, pieces, *refs),
        out_shape=[pltpu.VMEM(shape, jnp.float32)] * REACH,
        in_specs=[IN_SMEM] + [IN_VMEM] * (2 * pieces),
        out_specs=[IN_VMEM] * REACH,
        scratch_shapes=[pltpu.VMEM((REACH,) + shape, jnp.float32)],
        cost_estimate=pl.CostEstimate(
            flops=2 * pairs.shape[0] * shape[0] * shape[1] * order, bytes_accessed=40 * shape[0] * shape[1], transcendentals=0
        ),
        compiler_params=params(),
        name="pairs",
    )(pairs, *highs, *lows)


def shards(panel, diag_inverse, ancestor, live_blocks, pair_first, pair_second, pair_offset):
    me = lax.axis_index("grp").astype(jnp.int32)
    even = lax.axis_index("own") % 2 == 0
    mine, before = panel[0, 0], ancestor[0, 0]
    order = mine.shape[0]
    step = order // CHUNKS
    meta = jnp.concatenate([me[None], live_blocks])
    pairs = jnp.concatenate([pair_first[0, 0] ^ me, pair_second[0, 0] ^ me, pair_offset[0, 0]])
    factor = split_factor(meta, everyone(diag_inverse[0], "grp"))
    solved, highs, lows, done = [], [], [], {}
    for c in range(CHUNKS):
        panels = everyone(mine[c * step : (c + 1) * step], "grp")
        value, high, low = solve(meta, panels, factor)
        solved.append(value)
        highs.append(high)
        lows.append(low)
        sets = [((c,), tuple(range(c)))] if c else []
        sets.append((tuple(range(c + 1)), (c,)))
        for part, (left, right) in enumerate(sets):
            name = f"{c}{part}"
            outs = pair_sums(pairs, highs, lows, left, right)
            third = swapped(outs[3], "own", 1)
            first = swapped(outs[1], "own", 1)
            far = passed_along(outs[4] + jnp.where(even, third, 0.0), "own", 2)
            near = passed_along(far + outs[2] + jnp.where(even, first, third), "own", 2)
            rows = slice(left[0] * step, (left[-1] + 1) * step)
            cols = slice(right[0] * step, (right[-1] + 1) * step)
            done[name] = before[rows, cols] - (near + outs[0] + jnp.where(even, 0.0, first))
    updated = done["00"]
    for c in range(1, CHUNKS):
        below, beside = done[f"{c}0"], done[f"{c}1"]
        updated = jnp.concatenate([jnp.concatenate([updated, below], 0), beside], 1)
    return (jnp.concatenate(solved)[None, None], updated[None, None])


def solution(mesh):
    placed = (
        P("own", "grp", None, None),
        P("own", "grp", None),
        P("own", "grp", None, None),
        P("own"),
        P("own", "grp", None),
        P("own", "grp", None),
        P("own", "grp", None),
    )
    return jax.shard_map(
        shards,
        mesh=mesh,
        in_specs=placed,
        out_specs=(P("own", "grp", None, None), P("own", "grp", None, None)),
        check_vma=False,
    )
```
